32 devices in a mesh: row: 8 (over z, x), col: 4 (over y, core).
Axes of the slice: x: 2, y: 2, z: 4, core: 2. Of those that a mesh axis runs over, the one named last changes fastest.
Arguments:
- stream: bfloat16 [384, 8192], P('row', 'col'), may hold values from -6 to 6
- attention_gain: bfloat16 [8192], P('col'), may hold values from 0.25 to 1.75
- query_weight: bfloat16 [8192, 8192], P('col', 'row'), may hold values from -1 to 1
- pair_weight: bfloat16 [8192, 2048], P('col'), may hold values from -1 to 1
- out_weight: bfloat16 [8192, 8192], P('row', 'col'), may hold values from -0.0625 to 0.0625
- unit_gain: bfloat16 [8192], P('col'), may hold values from 0.25 to 1.75
- gate_weight: bfloat16 [8192, 24576], P('col', 'row'), may hold values from -0.0625 to 0.0625
- up_weight: bfloat16 [8192, 24576], P('col', 'row'), may hold values from -0.0625 to 0.0625
- down_weight: bfloat16 [24576, 8192], P('row', 'col'), may hold values from -0.0390625 to 0.0390625
Outputs:
- layer_out: bfloat16 [384, 8192], P('row', 'col')
The draws below stay inside these ranges and needn't reach their ends.
All inputs are finite; a program needn't handle non-finite values.
Results may differ from the reference program's by a relative error of at most 0.028.
Values may be sent and summed in bfloat16 or wider, within the bound.
A program may use at most 128 MiB of HBM per device.

```python
import jax
import jax.numpy as jnp
from jax import lax

D = 8192
HEADS = 64
KV_HEADS = 8
HD = 128
FF = 24576
TOKENS = 384
N_ROW = 8


def drawn_weight(key, width):
    values = jnp.clip(jax.random.normal(key, (D, width), jnp.float32), -5.0, 5.0)
    return values * D ** (-0.5)


def draw_stream(key, part):
    key_base = jax.random.fold_in(key, 1)
    key_rows = jax.random.fold_in(key, 2)
    spread = jnp.arange(D, dtype=jnp.float32) / D - 0.5
    column_scale = jnp.exp(2.302585 * spread)
    row_scale = jnp.exp(jax.random.uniform(key_rows, (TOKENS, 1), jnp.float32, -1.1513, 1.1513))
    base_values = jnp.clip(jax.random.normal(key_base, (TOKENS, D), jnp.float32), -5.0, 5.0)
    return (0.1 * base_values * row_scale * column_scale[None, :]).astype(jnp.bfloat16)


def draw_query_weight(key, part):
    width = HEADS * HD
    values = drawn_weight(jax.random.fold_in(key, 21), width)
    return values.astype(jnp.bfloat16)


def draw_pair_weight(key, part):
    width = 2 * KV_HEADS * HD
    values = drawn_weight(jax.random.fold_in(key, 31), width)
    return values.astype(jnp.bfloat16)


def levels(key, shape, cuts, low, top_value):
    loudness, own = 1.0, jax.random.fold_in(key, 6)
    for axis_at, shards_of in cuts:
        steps = jnp.exp(jax.random.uniform(jax.random.fold_in(own, axis_at), (shards_of,), jnp.float32, low / len(cuts), top_value / len(cuts)))
        loudness = loudness * jnp.repeat(steps, shape[axis_at] // shards_of).reshape([-1 if axis == axis_at else 1 for axis in range(len(shape))])
    return loudness


def centred(rng, shape, scale, reach, split=(), kind=jnp.bfloat16):
    loudness = levels(rng, shape, split, -0.22, 0.18) if split else 1.0
    array = jax.random.normal(rng, shape, jnp.float32) * scale * loudness
    return jnp.minimum(jnp.maximum(array, -reach), reach).astype(kind)


def setup_inputs(seed: int = 0) -> dict:
    seeds = jax.random.split(jax.random.key(seed), 10)
    stream = draw_stream(jax.random.fold_in(seeds[9], 71), 0)
    attention_gain = jnp.clip(1.0 + 0.15 * jax.random.normal(seeds[1], (D,), jnp.float32), 0.25, 1.75).astype(jnp.bfloat16)
    query_weight = draw_query_weight(jax.random.fold_in(seeds[9], 71), 0)
    pair_weight = draw_pair_weight(jax.random.fold_in(seeds[9], 71), 0)
    out_weight = centred(seeds[4], (HEADS * HD, D), (HEADS * HD) ** -0.5, 0.0625, ((0, 8), (1, 4)))
    unit_gain = jnp.clip(1.0 + 0.15 * jax.random.normal(seeds[5], (D,), jnp.float32), 0.25, 1.75).astype(jnp.bfloat16)
    gate_weight = centred(seeds[6], (D, FF), D ** -0.5, 0.0625, ((0, 4), (1, 8)))
    up_weight = centred(seeds[7], (D, FF), D ** -0.5, 0.0625, ((0, 4), (1, 8)))
    down_weight = centred(seeds[8], (FF, D), FF ** -0.5, 0.0390625, ((0, 8), (1, 4)))
    return {"stream": stream, "attention_gain": attention_gain, "query_weight": query_weight, "pair_weight": pair_weight, "out_weight": out_weight, "unit_gain": unit_gain, "gate_weight": gate_weight, "up_weight": up_weight, "down_weight": down_weight}


rope_base = 500000.0
epsilon = 1e-05

def rotate(values, positions):
    half_width = values.shape[-1] // 2
    frequency = rope_base ** (-(jnp.arange(half_width, dtype=jnp.float32) * 2.0 / values.shape[-1]))
    angles = positions.astype(jnp.float32)[:, None] * frequency[None, :]
    cosine = jnp.cos(angles)[:, None, :]
    sine_part = jnp.sin(angles)[:, None, :]
    first_part = values[..., :half_width]
    second = values[..., half_width:]
    return jnp.concatenate([first_part * cosine - second * sine_part, second * cosine + first_part * sine_part], axis=-1)

def rounded_blocks(left_side, weight, pieces):
    block_width = left_side.shape[1] // pieces
    left_blocks = left_side.reshape(left_side.shape[0], pieces, block_width).transpose(1, 0, 2)
    weight_blocks = weight.reshape(pieces, block_width, weight.shape[1])

    def accumulate(running, operands):
        product = jnp.dot(operands[0], operands[1], preferred_element_type=jnp.float32)
        rounded = lax.optimization_barrier(product.astype(jnp.bfloat16))
        return (running + rounded.astype(jnp.float32), None)
    running, unused = lax.scan(accumulate, jnp.zeros((left_side.shape[0], weight.shape[1]), jnp.float32), (left_blocks, weight_blocks))
    return running

def reference(stream, attention_gain, query_weight, pair_weight, out_weight, unit_gain, gate_weight, up_weight, down_weight):
    positions = jnp.arange(TOKENS, dtype=jnp.int32)
    stream_float = stream.astype(jnp.float32)
    attention_scale = lax.rsqrt(lax.optimization_barrier(jnp.sum(stream_float * stream_float, axis=1, keepdims=True)) / D + epsilon)
    normed = (stream_float * attention_gain.astype(jnp.float32)).astype(jnp.bfloat16)
    query_sums = jnp.dot(normed, query_weight, preferred_element_type=jnp.float32)
    pair_sums = jnp.dot(normed, pair_weight, preferred_element_type=jnp.float32)
    queries = rotate((attention_scale * query_sums).reshape(TOKENS, HEADS, HD), positions)
    key_value = (attention_scale * pair_sums).reshape(TOKENS, KV_HEADS, 2, HD)
    key_rows = rotate(key_value[:, :, 0, :], positions)
    value_rows = key_value[:, :, 1, :].astype(jnp.bfloat16)
    grouped = queries.reshape(TOKENS, KV_HEADS, HEADS // KV_HEADS, HD)
    scores = jnp.einsum('qhgd,khd->hgqk', grouped, key_rows, precision=lax.Precision.HIGHEST) * HD ** (-0.5)
    causal = positions[:, None] >= positions[None, :]
    scores = jnp.where(causal, scores, -1e+30)
    largest = lax.optimization_barrier(jnp.max(scores, axis=-1, keepdims=True))
    exponent = jnp.exp(scores - largest)
    attention = (exponent / lax.optimization_barrier(jnp.sum(exponent, axis=-1, keepdims=True))).astype(jnp.bfloat16)
    mixture = jnp.einsum('hgqk,khd->qhgd', attention.astype(jnp.float32), value_rows.astype(jnp.float32))
    heads_out = mixture.reshape(TOKENS, HEADS * HD).astype(jnp.bfloat16)
    attention_sums = rounded_blocks(heads_out, out_weight, N_ROW)
    hidden_stream = (stream_float + attention_sums).astype(jnp.bfloat16)
    hidden_float = hidden_stream.astype(jnp.float32)
    unit_scale = lax.rsqrt(lax.optimization_barrier(jnp.sum(hidden_float * hidden_float, axis=1, keepdims=True)) / D + epsilon)
    unit_input = (hidden_float * unit_gain.astype(jnp.float32)).astype(jnp.bfloat16)
    gate_sums = unit_scale * jnp.dot(unit_input, gate_weight, preferred_element_type=jnp.float32)
    upward = unit_scale * jnp.dot(unit_input, up_weight, preferred_element_type=jnp.float32)
    activated = (jax.nn.silu(gate_sums) * upward).astype(jnp.bfloat16)
    down_sums = rounded_blocks(activated, down_weight, N_ROW)
    return (hidden_float + down_sums).astype(jnp.bfloat16)
```

```python
import functools

import jax
import jax.numpy as jnp
from jax import lax
from jax.experimental import pallas as pl
from jax.experimental.pallas import tpu as pltpu
from jax.sharding import PartitionSpec as P

D = 8192
HEADS = 64
KV_HEADS = 8
HD = 128


rope_base = 500000.0
epsilon = 1e-05


def rotate(values, positions):
    half_width = values.shape[-1] // 2
    frequency = rope_base ** (-(jnp.arange(half_width, dtype=jnp.float32) * 2.0 / values.shape[-1]))
    angles = positions.astype(jnp.float32)[:, None] * frequency[None, :]
    cosine = jnp.cos(angles)[:, None, :]
    sine_part = jnp.sin(angles)[:, None, :]
    first_part = values[..., :half_width]
    second = values[..., half_width:]
    return jnp.concatenate(
        [first_part * cosine - second * sine_part, second * cosine + first_part * sine_part],
        axis=-1,
    )


def remote(axis, source, target, send_sem, recv_sem, device):
    return pltpu.make_async_remote_copy(
        src_ref=source,
        dst_ref=target,
        send_sem=send_sem,
        recv_sem=recv_sem,
        device_id={axis: device},
        device_id_type=pl.DeviceIdType.MESH,
    )


def greet(axis, me, line, depth):
    barrier = pltpu.get_barrier_semaphore()

    def signal(device):
        pl.semaphore_signal(
            barrier, inc=1, device_id={axis: device}, device_id_type=pl.DeviceIdType.MESH
        )

    signal(line * 2 + 1 - me % 2)
    pl.when(line < depth - 1)(lambda: signal(me + 2))
    pl.when(line > 0)(lambda: signal(me - 2))
    inner = (line > 0) & (line < depth - 1)
    pl.when(inner)(lambda: pl.semaphore_wait(barrier, 3))
    pl.when((line == 0) | (line == depth - 1))(lambda: pl.semaphore_wait(barrier, 2))


def gather_kernel(axis, depth, count, *refs):
    own, whole = refs[:count], refs[count : 2 * count]
    up_send, down_send, pair_send, line_recv, pair_recv = refs[2 * count :]
    me = lax.axis_index(axis)
    line, side = me // 2, me % 2
    partner = line * 2 + 1 - side
    greet(axis, me, line, depth)

    def up(k, at, source):
        block = whole[k].at[at * 2 + side]
        return remote(axis, source, block, up_send.at[k, at], line_recv.at[k, at], me + 2)

    def down(k, at, source):
        block = whole[k].at[at * 2 + side]
        return remote(axis, source, block, down_send.at[k, at], line_recv.at[k, at], me - 2)

    def across(k, at, source):
        block = whole[k].at[at * 2 + side]
        return remote(axis, source, block, pair_send.at[k, at], pair_recv.at[k, at], partner)

    for k in range(count):
        pl.when(line < depth - 1)(lambda k=k: up(k, line, own[k]).start())
        pl.when(line > 0)(lambda k=k: down(k, line, own[k]).start())
        across(k, line, own[k]).start()
    for k in range(count):
        whole[k][me] = own[k][...]
    for step in range(1, depth):

        @pl.when(line - step >= 0)
        def _():
            at = line - step
            for k in range(count):
                block = whole[k].at[at * 2 + side]
                remote(
                    axis, block, block, up_send.at[k, at], line_recv.at[k, at], partner
                ).wait_recv()
                pl.when(line < depth - 1)(lambda k=k, block=block: up(k, at, block).start())
                across(k, at, block).start()

        @pl.when(line + step < depth)
        def _():
            at = line + step
            for k in range(count):
                block = whole[k].at[at * 2 + side]
                remote(
                    axis, block, block, down_send.at[k, at], line_recv.at[k, at], partner
                ).wait_recv()
                pl.when(line > 0)(lambda k=k, block=block: down(k, at, block).start())
                across(k, at, block).start()

    for at in range(depth):
        for k in range(count):
            block = whole[k].at[at * 2 + 1 - side]
            sent = whole[k].at[at * 2 + side]
            remote(axis, block, block, pair_send.at[k, at], pair_recv.at[k, at], partner).wait_recv()
            across(k, at, sent).wait_send()
            pl.when((line < depth - 1) & (line >= at))(
                lambda k=k, at=at, sent=sent: up(k, at, sent).wait_send()
            )
            pl.when((line > 0) & (line <= at))(
                lambda k=k, at=at, sent=sent: down(k, at, sent).wait_send()
            )


def scatter_kernel(axis, depth, count, *refs):
    parts, totals = refs[:count], refs[count : 2 * count]
    taken, sums, passed = (refs[(2 + i) * count : (3 + i) * count] for i in range(3))
    pair_send, pair_recv, line_send, line_recv = refs[5 * count :]
    me = lax.axis_index(axis)
    line, side = me // 2, me % 2
    partner = line * 2 + 1 - side
    greet(axis, me, line, depth)

    def across(k, at):
        return remote(
            axis,
            parts[k].at[at * 2 + 1 - side],
            taken[k].at[at],
            pair_send.at[k, at],
            pair_recv.at[k, at],
            partner,
        )

    def along(k, at, slot, device):
        return remote(
            axis,
            sums[k].at[at],
            passed[k].at[slot],
            line_send.at[k, at],
            line_recv.at[k, slot],
            device,
        )

    def add(k, at, slots, target):
        rows = parts[k].shape[1]
        piece = 16 if rows % 16 == 0 else rows

        def body(i, carry):
            here = pl.ds(pl.multiple_of(i * piece, piece), piece)
            value = parts[k][at * 2 + side, here].astype(jnp.float32)
            value = value + taken[k][at, here].astype(jnp.float32)
            for slot in slots:
                value = value + passed[k][slot, here].astype(jnp.float32)
            target[here] = value.astype(target.dtype)
            return carry

        lax.fori_loop(0, rows // piece, body, 0)

    for step in range(depth - 1, 0, -1):

        @pl.when(line + step < depth)
        def _():
            for k in range(count):
                across(k, line + step).start()

        @pl.when(line - step >= 0)
        def _():
            for k in range(count):
                across(k, line - step).start()

    for k in range(count):
        across(k, line).start()

    for step in range(depth - 1, 0, -1):

        @pl.when(line + step < depth)
        def _():
            at = line + step
            for k in range(count):
                across(k, at).wait_recv()

                @pl.when(line > 0)
                def _():
                    along(k, at, at, partner).wait_recv()
                    add(k, at, (at,), sums[k].at[at])

                @pl.when(line == 0)
                def _():
                    add(k, at, (), sums[k].at[at])

                along(k, at, at, me + 2).start()

        @pl.when(line - step >= 0)
        def _():
            at = line - step
            slot = at if step > 1 else depth
            for k in range(count):
                across(k, at).wait_recv()

                @pl.when(line < depth - 1)
                def _():
                    along(k, at, at, partner).wait_recv()
                    add(k, at, (at,), sums[k].at[at])

                @pl.when(line == depth - 1)
                def _():
                    add(k, at, (), sums[k].at[at])

                along(k, at, slot, me - 2).start()

    for k in range(count):
        across(k, line).wait_recv()

        @pl.when(line == 0)
        def _():
            along(k, line, depth, partner).wait_recv()
            add(k, line, (depth,), totals[k])

        @pl.when(line == depth - 1)
        def _():
            along(k, line, line, partner).wait_recv()
            add(k, line, (line,), totals[k])

        @pl.when((line > 0) & (line < depth - 1))
        def _():
            along(k, line, line, partner).wait_recv()
            along(k, line, depth, partner).wait_recv()
            add(k, line, (line, depth), totals[k])

    for at in range(depth):
        for k in range(count):
            across(k, at).wait_send()
            pl.when(line != at)(lambda k=k, at=at: along(k, at, at, partner).wait_send())


def call(kernel, results, arrays, scratch, number):
    in_vmem = pl.BlockSpec(memory_space=pltpu.VMEM)
    return pl.pallas_call(
        kernel,
        out_shape=results,
        in_specs=[in_vmem] * len(arrays),
        out_specs=[in_vmem] * len(results),
        scratch_shapes=scratch,
        compiler_params=pltpu.CompilerParams(collective_id=number, has_side_effects=True),
    )(*arrays)


def gather(axis, number, *arrays):
    size = lax.axis_size(axis)
    depth, count = size // 2, len(arrays)
    semaphores = [pltpu.SemaphoreType.DMA((count, depth))] * 5
    results = [jax.ShapeDtypeStruct((size,) + a.shape, a.dtype) for a in arrays]
    whole = call(
        functools.partial(gather_kernel, axis, depth, count), results, arrays, semaphores, number
    )
    return [w.reshape((size * a.shape[0],) + a.shape[1:]) for w, a in zip(whole, arrays)]


def scatter(axis, number, *arrays):
    size = lax.axis_size(axis)
    depth, count = size // 2, len(arrays)
    parts = [a.reshape((size, a.shape[0] // size) + a.shape[1:]) for a in arrays]
    scratch = [
        pltpu.VMEM((slots,) + p.shape[1:], p.dtype)
        for slots in (depth, depth, depth + 1)
        for p in parts
    ]
    scratch += [pltpu.SemaphoreType.DMA((count, depth))] * 3
    scratch += [pltpu.SemaphoreType.DMA((count, depth + 1))]
    results = [jax.ShapeDtypeStruct(p.shape[1:], jnp.float32) for p in parts]
    return call(
        functools.partial(scatter_kernel, axis, depth, count), results, parts, scratch, number
    )


def product(left_side, weight):
    return jnp.dot(left_side, weight, preferred_element_type=jnp.float32).astype(jnp.bfloat16)


def square_sums(values):
    sums = jnp.sum(values * values, axis=1, keepdims=True)
    return jnp.broadcast_to(sums, (values.shape[0], 128))


def on_device(
    stream,
    attention_gain,
    query_weight,
    pair_weight,
    out_weight,
    unit_gain,
    gate_weight,
    up_weight,
    down_weight,
):
    row_index = lax.axis_index("row")
    column_index = lax.axis_index("col")
    (every_token,) = gather("row", 0, stream)
    tokens = every_token.shape[0]
    query_count = tokens // lax.axis_size("col")
    heads_here = query_weight.shape[1] // HD
    query_width = heads_here * HD
    pair_head = row_index * heads_here // (HEADS // KV_HEADS)
    whole_float = every_token.astype(jnp.float32)
    normed = (whole_float * attention_gain.astype(jnp.float32)).astype(jnp.bfloat16)
    pair_columns = lax.dynamic_slice_in_dim(pair_weight, pair_head * 2 * HD, 2 * HD, 1)
    query_rows, pair_sums, squares = scatter(
        "col",
        1,
        product(normed, query_weight),
        product(normed, pair_columns),
        square_sums(whole_float),
    )
    query_start = column_index * query_count
    row_scale = lax.rsqrt(squares[:, :1] / D + epsilon)
    positions = jnp.arange(tokens, dtype=jnp.int32)
    query_positions = query_start + jnp.arange(query_count, dtype=jnp.int32)
    queries = rotate((row_scale * query_rows).reshape(query_count, heads_here, HD), query_positions)
    pair_values = row_scale * pair_sums
    own_keys = rotate(pair_values[:, :HD].reshape(query_count, 1, HD), query_positions)[:, 0, :]
    own_values = pair_values[:, HD:].astype(jnp.bfloat16)
    key_rows, value_rows = gather("col", 2, own_keys, own_values)
    scores = jnp.einsum("qhd,kd->hqk", queries, key_rows, precision=lax.Precision.HIGHEST) * HD ** (
        -0.5
    )
    causal = query_positions[:, None] >= positions[None, :]
    scores = jnp.where(causal[None, :, :], scores, -1e30)
    largest = jnp.max(scores, axis=-1, keepdims=True)
    exponent = jnp.exp(scores - largest)
    attention = (exponent / jnp.sum(exponent, axis=-1, keepdims=True)).astype(jnp.bfloat16)
    mixture = jnp.einsum("hqk,kd->qhd", attention, value_rows, preferred_element_type=jnp.float32)
    heads_out = mixture.reshape(query_count, query_width).astype(jnp.bfloat16)
    (every_head,) = gather("col", 3, heads_out)
    (attention_rows,) = scatter("row", 4, product(every_head, out_weight))
    hidden_rows = (stream.astype(jnp.float32) + attention_rows).astype(jnp.bfloat16)
    (hidden_all,) = gather("row", 5, hidden_rows)
    hidden_float = hidden_all.astype(jnp.float32)
    unit_input = (hidden_float * unit_gain.astype(jnp.float32)).astype(jnp.bfloat16)
    gate_rows, up_rows, square_rows = scatter(
        "col",
        6,
        product(unit_input, gate_weight),
        product(unit_input, up_weight),
        square_sums(hidden_float),
    )
    unit_scale = lax.rsqrt(square_rows[:, :1] / D + epsilon)
    gate_sums = unit_scale * gate_rows
    upward = unit_scale * up_rows
    (activated,) = gather("col", 7, (jax.nn.silu(gate_sums) * upward).astype(jnp.bfloat16))
    (down_rows,) = scatter("row", 8, product(activated, down_weight))
    return (hidden_rows.astype(jnp.float32) + down_rows).astype(jnp.bfloat16)


def solution(mesh):
    return jax.shard_map(
        on_device,
        mesh=mesh,
        in_specs=(
            P("row", "col"),
            P("col"),
            P("col", "row"),
            P("col", None),
            P("row", "col"),
            P("col"),
            P("col", "row"),
            P("col", "row"),
            P("row", "col"),
        ),
        out_specs=P("row", "col"),
        check_vma=False,
    )
```

```python
import functools

import jax
import jax.numpy as jnp
from jax import lax
from jax.experimental import pallas as pl
from jax.experimental.pallas import tpu as pltpu
from jax.sharding import PartitionSpec as P

D = 8192
HEADS = 64
KV_HEADS = 8
HD = 128


rope_base = 500000.0
epsilon = 1e-05


def rotate(values, positions):
    half_width = values.shape[-1] // 2
    frequency = rope_base ** (-(jnp.arange(half_width, dtype=jnp.float32) * 2.0 / values.shape[-1]))
    angles = positions.astype(jnp.float32)[:, None] * frequency[None, :]
    cosine = jnp.cos(angles)[:, None, :]
    sine_part = jnp.sin(angles)[:, None, :]
    first_part = values[..., :half_width]
    second = values[..., half_width:]
    return jnp.concatenate(
        [first_part * cosine - second * sine_part, second * cosine + first_part * sine_part],
        axis=-1,
    )


def remote(axis, source, target, send_sem, recv_sem, device):
    return pltpu.make_async_remote_copy(
        src_ref=source,
        dst_ref=target,
        send_sem=send_sem,
        recv_sem=recv_sem,
        device_id={axis: device},
        device_id_type=pl.DeviceIdType.MESH,
    )


def greet(axis, me, line, depth):
    barrier = pltpu.get_barrier_semaphore()

    def signal(device):
        pl.semaphore_signal(
            barrier, inc=1, device_id={axis: device}, device_id_type=pl.DeviceIdType.MESH
        )

    signal(line * 2 + 1 - me % 2)
    pl.when(line < depth - 1)(lambda: signal(me + 2))
    pl.when(line > 0)(lambda: signal(me - 2))
    inner = (line > 0) & (line < depth - 1)
    pl.when(inner)(lambda: pl.semaphore_wait(barrier, 3))
    pl.when((line == 0) | (line == depth - 1))(lambda: pl.semaphore_wait(barrier, 2))


def cut(shape, dtype):
    rows, most = shape[0] // 16, shape[0] * shape[1] * jnp.dtype(dtype).itemsize // 49152
    if shape[0] % 16:
        return 1
    return max(p for p in range(1, rows + 1) if rows % p == 0 and p <= max(most, 1))


def views(refs, pieces):
    return [
        ref.at[:, pl.ds(i * (ref.shape[1] // runs), ref.shape[1] // runs)]
        for ref, runs in zip(refs, pieces)
        for i in range(runs)
    ]


def gather_kernel(axis, depth, pieces, *refs):
    count = len(pieces)
    kept, full = refs[:count], refs[count : 2 * count]
    up_send, down_send, pair_send, line_recv, pair_recv = refs[2 * count :]
    own = [view.at[0] for view in views(kept, pieces)]
    whole = views(full, pieces)
    count = len(whole)
    me = lax.axis_index(axis)
    line, side = me // 2, me % 2
    partner = line * 2 + 1 - side
    greet(axis, me, line, depth)

    def up(k, at, source):
        block = whole[k].at[at * 2 + side]
        return remote(axis, source, block, up_send.at[k, at], line_recv.at[k, at], me + 2)

    def down(k, at, source):
        block = whole[k].at[at * 2 + side]
        return remote(axis, source, block, down_send.at[k, at], line_recv.at[k, at], me - 2)

    def across(k, at, source):
        block = whole[k].at[at * 2 + side]
        return remote(axis, source, block, pair_send.at[k, at], pair_recv.at[k, at], partner)

    for k in range(count):
        pl.when(line < depth - 1)(lambda k=k: up(k, line, own[k]).start())
        pl.when(line > 0)(lambda k=k: down(k, line, own[k]).start())
        across(k, line, own[k]).start()
    for source, target in zip(kept, full):
        target[me] = source[0]
    def pass_on(k, at, more, send):
        block = whole[k].at[at * 2 + side]
        remote(
            axis, block, block, pair_send.at[k, at], line_recv.at[k, at], partner
        ).wait_recv()
        pl.when(more)(lambda: send(k, at, block).start())
        across(k, at, block).start()

    for step in range(1, depth):
        for k in range(count):
            pl.when(line - step >= 0)(lambda: pass_on(k, line - step, line < depth - 1, up))
            pl.when(line + step < depth)(lambda: pass_on(k, line + step, line > 0, down))

    for at in range(depth):
        for k in range(count):
            block = whole[k].at[at * 2 + 1 - side]
            sent = whole[k].at[at * 2 + side]
            remote(axis, block, block, pair_send.at[k, at], pair_recv.at[k, at], partner).wait_recv()
            across(k, at, sent).wait_send()
            pl.when((line < depth - 1) & (line >= at))(
                lambda k=k, at=at, sent=sent: up(k, at, sent).wait_send()
            )
            pl.when((line > 0) & (line <= at))(
                lambda k=k, at=at, sent=sent: down(k, at, sent).wait_send()
            )


def scatter_kernel(axis, depth, pieces, *refs):
    count = len(pieces)
    parts, totals, taken, sums, passed = (
        views(refs[i * count : (i + 1) * count], pieces) for i in range(5)
    )
    pair_send, pair_recv, line_send, line_recv = refs[5 * count :]
    count = len(parts)
    me = lax.axis_index(axis)
    line, side = me // 2, me % 2
    partner = line * 2 + 1 - side
    greet(axis, me, line, depth)

    def across(k, at):
        return remote(
            axis,
            parts[k].at[at * 2 + 1 - side],
            taken[k].at[at],
            pair_send.at[k, at],
            pair_recv.at[k, at],
            partner,
        )

    def along(k, at, slot, device):
        return remote(
            axis,
            sums[k].at[at],
            passed[k].at[slot],
            line_send.at[k, at],
            line_recv.at[k, slot],
            device,
        )

    def add(k, at, slots, target):
        rows = target.shape[0]
        piece = 16 if rows % 16 == 0 else rows

        def body(i, carry):
            here = pl.ds(pl.multiple_of(i * piece, piece), piece)
            value = parts[k][at * 2 + side, here].astype(jnp.float32)
            value = value + taken[k][at, here].astype(jnp.float32)
            for slot in slots:
                value = value + passed[k][slot, here].astype(jnp.float32)
            target[here] = value.astype(target.dtype)
            return carry

        lax.fori_loop(0, rows // piece, body, 0)

    for step in range(depth - 1, 0, -1):
        for k in range(count):
            pl.when(line + step < depth)(lambda: across(k, line + step).start())
            pl.when(line - step >= 0)(lambda: across(k, line - step).start())

    for k in range(count):
        across(k, line).start()

    def pass_on(k, at, first, slot, device):
        across(k, at).wait_recv()

        @pl.when(jnp.logical_not(first))
        def _():
            along(k, at, at, partner).wait_recv()
            add(k, at, (at,), sums[k].at[at])

        @pl.when(first)
        def _():
            add(k, at, (), sums[k].at[at])

        along(k, at, slot, device).start()

    for step in range(depth - 1, 0, -1):
        for k in range(count):

            @pl.when(line + step < depth)
            def _():
                pass_on(k, line + step, line == 0, line + step, me + 2)

            @pl.when(line - step >= 0)
            def _():
                slot = line - step if step > 1 else depth
                pass_on(k, line - step, line == depth - 1, slot, me - 2)

    for k in range(count):
        across(k, line).wait_recv()

        @pl.when(line == 0)
        def _():
            along(k, line, depth, partner).wait_recv()
            add(k, line, (depth,), totals[k].at[0])

        @pl.when(line == depth - 1)
        def _():
            along(k, line, line, partner).wait_recv()
            add(k, line, (line,), totals[k].at[0])

        @pl.when((line > 0) & (line < depth - 1))
        def _():
            along(k, line, line, partner).wait_recv()
            along(k, line, depth, partner).wait_recv()
            add(k, line, (line, depth), totals[k].at[0])

    for at in range(depth):
        for k in range(count):
            across(k, at).wait_send()
            pl.when(line != at)(lambda k=k, at=at: along(k, at, at, partner).wait_send())


def call(kernel, results, arrays, scratch, number):
    in_vmem = pl.BlockSpec(memory_space=pltpu.VMEM)
    return pl.pallas_call(
        kernel,
        out_shape=results,
        in_specs=[in_vmem] * len(arrays),
        out_specs=[in_vmem] * len(results),
        scratch_shapes=scratch,
        compiler_params=pltpu.CompilerParams(collective_id=number, has_side_effects=True),
    )(*arrays)


def gather(axis, number, *arrays):
    size = lax.axis_size(axis)
    depth, pieces = size // 2, [cut(a.shape, a.dtype) for a in arrays]
    semaphores = [pltpu.SemaphoreType.DMA((sum(pieces), depth))] * 5
    results = [jax.ShapeDtypeStruct((size,) + a.shape, a.dtype) for a in arrays]
    whole = call(
        functools.partial(gather_kernel, axis, depth, pieces),
        results,
        [a[None] for a in arrays],
        semaphores,
        number,
    )
    return [w.reshape((size * a.shape[0],) + a.shape[1:]) for w, a in zip(whole, arrays)]


def scatter(axis, number, *arrays):
    size = lax.axis_size(axis)
    depth = size // 2
    parts = [a.reshape((size, a.shape[0] // size) + a.shape[1:]) for a in arrays]
    pieces = [cut(p.shape[1:], p.dtype) for p in parts]
    count = sum(pieces)
    scratch = [
        pltpu.VMEM((slots,) + p.shape[1:], p.dtype)
        for slots in (depth, depth, depth + 1)
        for p in parts
    ]
    scratch += [pltpu.SemaphoreType.DMA((count, depth))] * 3
    scratch += [pltpu.SemaphoreType.DMA((count, depth + 1))]
    results = [jax.ShapeDtypeStruct((1,) + p.shape[1:], jnp.float32) for p in parts]
    sums = call(
        functools.partial(scatter_kernel, axis, depth, pieces), results, parts, scratch, number
    )
    return [s[0] for s in sums]


def product(left_side, weight):
    return jnp.dot(left_side, weight, preferred_element_type=jnp.float32).astype(jnp.bfloat16)


def square_sums(values):
    sums = jnp.sum(values * values, axis=1, keepdims=True)
    return jnp.broadcast_to(sums, (values.shape[0], 128))


def on_device(
    stream,
    attention_gain,
    query_weight,
    pair_weight,
    out_weight,
    unit_gain,
    gate_weight,
    up_weight,
    down_weight,
):
    row_index = lax.axis_index("row")
    column_index = lax.axis_index("col")
    (every_token,) = gather("row", 0, stream)
    tokens = every_token.shape[0]
    query_count = tokens // lax.axis_size("col")
    heads_here = query_weight.shape[1] // HD
    query_width = heads_here * HD
    pair_head = row_index * heads_here // (HEADS // KV_HEADS)
    whole_float = every_token.astype(jnp.float32)
    normed = (whole_float * attention_gain.astype(jnp.float32)).astype(jnp.bfloat16)
    pair_columns = lax.dynamic_slice_in_dim(pair_weight, pair_head * 2 * HD, 2 * HD, 1)
    query_rows, pair_sums, squares = scatter(
        "col",
        1,
        product(normed, query_weight),
        product(normed, pair_columns),
        square_sums(whole_float),
    )
    query_start = column_index * query_count
    row_scale = lax.rsqrt(squares[:, :1] / D + epsilon)
    positions = jnp.arange(tokens, dtype=jnp.int32)
    query_positions = query_start + jnp.arange(query_count, dtype=jnp.int32)
    queries = rotate((row_scale * query_rows).reshape(query_count, heads_here, HD), query_positions)
    pair_values = row_scale * pair_sums
    own_keys = rotate(pair_values[:, :HD].reshape(query_count, 1, HD), query_positions)[:, 0, :]
    own_values = pair_values[:, HD:].astype(jnp.bfloat16)
    key_rows, value_rows = gather("col", 2, own_keys, own_values)
    scores = jnp.einsum("qhd,kd->hqk", queries, key_rows, precision=lax.Precision.HIGHEST) * HD ** (
        -0.5
    )
    causal = query_positions[:, None] >= positions[None, :]
    scores = jnp.where(causal[None, :, :], scores, -1e30)
    largest = jnp.max(scores, axis=-1, keepdims=True)
    exponent = jnp.exp(scores - largest)
    attention = (exponent / jnp.sum(exponent, axis=-1, keepdims=True)).astype(jnp.bfloat16)
    mixture = jnp.einsum("hqk,kd->qhd", attention, value_rows, preferred_element_type=jnp.float32)
    heads_out = mixture.reshape(query_count, query_width).astype(jnp.bfloat16)
    (every_head,) = gather("col", 3, heads_out)
    (attention_rows,) = scatter("row", 4, product(every_head, out_weight))
    hidden_rows = (stream.astype(jnp.float32) + attention_rows).astype(jnp.bfloat16)
    (hidden_all,) = gather("row", 5, hidden_rows)
    hidden_float = hidden_all.astype(jnp.float32)
    unit_input = (hidden_float * unit_gain.astype(jnp.float32)).astype(jnp.bfloat16)
    gate_rows, up_rows, square_rows = scatter(
        "col",
        6,
        product(unit_input, gate_weight),
        product(unit_input, up_weight),
        square_sums(hidden_float),
    )
    unit_scale = lax.rsqrt(square_rows[:, :1] / D + epsilon)
    gate_sums = unit_scale * gate_rows
    upward = unit_scale * up_rows
    (activated,) = gather("col", 7, (jax.nn.silu(gate_sums) * upward).astype(jnp.bfloat16))
    (down_rows,) = scatter("row", 8, product(activated, down_weight))
    return (hidden_rows.astype(jnp.float32) + down_rows).astype(jnp.bfloat16)


def solution(mesh):
    return jax.shard_map(
        on_device,
        mesh=mesh,
        in_specs=(
            P("row", "col"),
            P("col"),
            P("col", "row"),
            P("col", None),
            P("row", "col"),
            P("col"),
            P("col", "row"),
            P("col", "row"),
            P("row", "col"),
        ),
        out_specs=P("row", "col"),
        check_vma=False,
    )
```

```python
import functools

import jax
import jax.numpy as jnp
from jax import lax
from jax.experimental import pallas as pl
from jax.experimental.pallas import tpu as pltpu
from jax.sharding import PartitionSpec as P

D = 8192
HEADS = 64
KV_HEADS = 8
HD = 128


rope_base = 500000.0
epsilon = 1e-05


def rotate(values, positions):
    half_width = values.shape[-1] // 2
    frequency = rope_base ** (-(jnp.arange(half_width, dtype=jnp.float32) * 2.0 / values.shape[-1]))
    angles = positions.astype(jnp.float32)[:, None] * frequency[None, :]
    cosine = jnp.cos(angles)[:, None, :]
    sine_part = jnp.sin(angles)[:, None, :]
    first_part = values[..., :half_width]
    second = values[..., half_width:]
    return jnp.concatenate(
        [first_part * cosine - second * sine_part, second * cosine + first_part * sine_part],
        axis=-1,
    )


def remote(axis, source, target, send_sem, recv_sem, device):
    return pltpu.make_async_remote_copy(
        src_ref=source,
        dst_ref=target,
        send_sem=send_sem,
        recv_sem=recv_sem,
        device_id={axis: device},
        device_id_type=pl.DeviceIdType.MESH,
    )


def greet(axis, me, line, depth):
    barrier = pltpu.get_barrier_semaphore()

    def signal(device):
        pl.semaphore_signal(
            barrier, inc=1, device_id={axis: device}, device_id_type=pl.DeviceIdType.MESH
        )

    signal(line * 2 + 1 - me % 2)
    pl.when(line < depth - 1)(lambda: signal(me + 2))
    pl.when(line > 0)(lambda: signal(me - 2))
    inner = (line > 0) & (line < depth - 1)
    pl.when(inner)(lambda: pl.semaphore_wait(barrier, 3))
    pl.when((line == 0) | (line == depth - 1))(lambda: pl.semaphore_wait(barrier, 2))


def cut(shape, dtype):
    rows, most = shape[0] // 16, shape[0] * shape[1] * jnp.dtype(dtype).itemsize // 49152
    if shape[0] % 16:
        return 1
    return max(p for p in range(1, rows + 1) if rows % p == 0 and p <= max(most, 1))


def views(refs, pieces):
    return [
        ref.at[:, pl.ds(i * (ref.shape[1] // runs), ref.shape[1] // runs)]
        for ref, runs in zip(refs, pieces)
        for i in range(runs)
    ]


def gather_kernel(axis, depth, pieces, *refs):
    count = len(pieces)
    kept, full = refs[:count], refs[count : 2 * count]
    up_send, down_send, pair_send, line_recv, pair_recv = refs[2 * count :]
    own = [view.at[0] for view in views(kept, pieces)]
    whole = views(full, pieces)
    count = len(whole)
    me = lax.axis_index(axis)
    line, side = me // 2, me % 2
    partner = line * 2 + 1 - side
    greet(axis, me, line, depth)

    def up(k, at, source):
        block = whole[k].at[at * 2 + side]
        return remote(axis, source, block, up_send.at[k, at], line_recv.at[k, at], me + 2)

    def down(k, at, source):
        block = whole[k].at[at * 2 + side]
        return remote(axis, source, block, down_send.at[k, at], line_recv.at[k, at], me - 2)

    def across(k, at, source):
        block = whole[k].at[at * 2 + side]
        return remote(axis, source, block, pair_send.at[k, at], pair_recv.at[k, at], partner)

    for k in range(count):
        pl.when(line < depth - 1)(lambda k=k: up(k, line, own[k]).start())
        pl.when(line > 0)(lambda k=k: down(k, line, own[k]).start())
        across(k, line, own[k]).start()
    for source, target in zip(kept, full):
        target[me] = source[0]
    def pass_on(k, at, more, send):
        block = whole[k].at[at * 2 + side]
        remote(
            axis, block, block, pair_send.at[k, at], line_recv.at[k, at], partner
        ).wait_recv()
        pl.when(more)(lambda: send(k, at, block).start())
        across(k, at, block).start()

    for step in range(1, depth):
        for k in range(count):
            pl.when(line - step >= 0)(lambda: pass_on(k, line - step, line < depth - 1, up))
            pl.when(line + step < depth)(lambda: pass_on(k, line + step, line > 0, down))

    for at in range(depth):
        for k in range(count):
            block = whole[k].at[at * 2 + 1 - side]
            sent = whole[k].at[at * 2 + side]
            remote(axis, block, block, pair_send.at[k, at], pair_recv.at[k, at], partner).wait_recv()
            across(k, at, sent).wait_send()
            pl.when((line < depth - 1) & (line >= at))(
                lambda k=k, at=at, sent=sent: up(k, at, sent).wait_send()
            )
            pl.when((line > 0) & (line <= at))(
                lambda k=k, at=at, sent=sent: down(k, at, sent).wait_send()
            )


def multiply(left, weight, made):
    size, rows, width = made.shape
    tile = 256 if width % 256 == 0 else width

    def body(i, carry):
        columns = pl.ds(pl.multiple_of(i * tile, tile), tile)
        value = jnp.dot(left[...], weight[:, columns], preferred_element_type=jnp.float32)
        for b in range(size):
            made[b, :, columns] = value[b * rows : (b + 1) * rows].astype(made.dtype)
        return carry

    lax.fori_loop(0, width // tile, body, 0)


def scatter_kernel(axis, depth, pieces, late, *refs):
    count = len(pieces)
    given, refs = refs[: count - late], refs[count - late :]
    operands, refs = refs[: 2 * late], refs[2 * late :]
    results, refs = refs[:count], refs[count:]
    made, refs = refs[:late], refs[late:]
    parts, totals = views(given + made, pieces), views(results, pieces)
    taken, sums, passed = (
        views(refs[i * count : (i + 1) * count], pieces) for i in range(3)
    )
    pair_send, pair_recv, line_send, line_recv = refs[3 * count :]
    count = len(parts)
    me = lax.axis_index(axis)
    line, side = me // 2, me % 2
    partner = line * 2 + 1 - side
    greet(axis, me, line, depth)

    def across(k, at):
        return remote(
            axis,
            parts[k].at[at * 2 + 1 - side],
            taken[k].at[at],
            pair_send.at[k, at],
            pair_recv.at[k, at],
            partner,
        )

    def along(k, at, slot, device):
        return remote(
            axis,
            sums[k].at[at],
            passed[k].at[slot],
            line_send.at[k, at],
            line_recv.at[k, slot],
            device,
        )

    def add(k, at, slots, target):
        rows = target.shape[0]
        piece = 16 if rows % 16 == 0 else rows

        def body(i, carry):
            here = pl.ds(pl.multiple_of(i * piece, piece), piece)
            value = parts[k][at * 2 + side, here].astype(jnp.float32)
            value = value + taken[k][at, here].astype(jnp.float32)
            for slot in slots:
                value = value + passed[k][slot, here].astype(jnp.float32)
            target[here] = value.astype(target.dtype)
            return carry

        lax.fori_loop(0, rows // piece, body, 0)

    def pass_on(k, at, first, slot, device):
        across(k, at).wait_recv()

        @pl.when(jnp.logical_not(first))
        def _():
            along(k, at, at, partner).wait_recv()
            add(k, at, (at,), sums[k].at[at])

        @pl.when(first)
        def _():
            add(k, at, (), sums[k].at[at])

        along(k, at, slot, device).start()

    def travel(turns):
        for step in range(depth - 1, 0, -1):
            for k in turns:
                pl.when(line + step < depth)(lambda: across(k, line + step).start())
                pl.when(line - step >= 0)(lambda: across(k, line - step).start())
        for k in turns:
            across(k, line).start()
        for step in range(depth - 1, 0, -1):
            for k in turns:

                @pl.when(line + step < depth)
                def _():
                    pass_on(k, line + step, line == 0, line + step, me + 2)

                @pl.when(line - step >= 0)
                def _():
                    slot = line - step if step > 1 else depth
                    pass_on(k, line - step, line == depth - 1, slot, me - 2)

    ready = count - pieces[-1] if late else count
    travel(range(ready))
    if late:
        multiply(*operands, *made)
        travel(range(ready, count))

    for k in range(count):
        across(k, line).wait_recv()

        @pl.when(line == 0)
        def _():
            along(k, line, depth, partner).wait_recv()
            add(k, line, (depth,), totals[k].at[0])

        @pl.when(line == depth - 1)
        def _():
            along(k, line, line, partner).wait_recv()
            add(k, line, (line,), totals[k].at[0])

        @pl.when((line > 0) & (line < depth - 1))
        def _():
            along(k, line, line, partner).wait_recv()
            along(k, line, depth, partner).wait_recv()
            add(k, line, (line, depth), totals[k].at[0])

    for at in range(depth):
        for k in range(count):
            across(k, at).wait_send()
            pl.when(line != at)(lambda k=k, at=at: along(k, at, at, partner).wait_send())


def call(kernel, results, arrays, scratch, number):
    in_vmem = pl.BlockSpec(memory_space=pltpu.VMEM)
    return pl.pallas_call(
        kernel,
        out_shape=results,
        in_specs=[in_vmem] * len(arrays),
        out_specs=[in_vmem] * len(results),
        scratch_shapes=scratch,
        compiler_params=pltpu.CompilerParams(collective_id=number, has_side_effects=True),
    )(*arrays)


def gather(axis, number, *arrays):
    size = lax.axis_size(axis)
    depth, pieces = size // 2, [cut(a.shape, a.dtype) for a in arrays]
    semaphores = [pltpu.SemaphoreType.DMA((sum(pieces), depth))] * 5
    results = [jax.ShapeDtypeStruct((size,) + a.shape, a.dtype) for a in arrays]
    whole = call(
        functools.partial(gather_kernel, axis, depth, pieces),
        results,
        [a[None] for a in arrays],
        semaphores,
        number,
    )
    return [w.reshape((size * a.shape[0],) + a.shape[1:]) for w, a in zip(whole, arrays)]


def scatter(axis, number, *arrays, late=()):
    size = lax.axis_size(axis)
    depth = size // 2
    parts = [a.reshape((size, a.shape[0] // size) + a.shape[1:]) for a in arrays]
    blocks = [jax.ShapeDtypeStruct(p.shape, p.dtype) for p in parts]
    if late:
        shape = (size, late[0].shape[0] // size, late[1].shape[1])
        blocks.append(jax.ShapeDtypeStruct(shape, jnp.bfloat16))
    pieces = [cut(p.shape[1:], p.dtype) for p in blocks]
    count = sum(pieces)
    scratch = [pltpu.VMEM(shape, jnp.bfloat16)] if late else []
    scratch += [
        pltpu.VMEM((slots,) + p.shape[1:], p.dtype)
        for slots in (depth, depth, depth + 1)
        for p in blocks
    ]
    scratch += [pltpu.SemaphoreType.DMA((count, depth))] * 3
    scratch += [pltpu.SemaphoreType.DMA((count, depth + 1))]
    results = [jax.ShapeDtypeStruct((1,) + p.shape[1:], jnp.float32) for p in blocks]
    sums = call(
        functools.partial(scatter_kernel, axis, depth, pieces, len(late) // 2),
        results,
        [*parts, *late],
        scratch,
        number,
    )
    return [s[0] for s in sums]


def product(left_side, weight):
    return jnp.dot(left_side, weight, preferred_element_type=jnp.float32).astype(jnp.bfloat16)


def square_sums(values):
    sums = jnp.sum(values * values, axis=1, keepdims=True)
    return jnp.broadcast_to(sums, (values.shape[0], 128))


def on_device(
    stream,
    attention_gain,
    query_weight,
    pair_weight,
    out_weight,
    unit_gain,
    gate_weight,
    up_weight,
    down_weight,
):
    row_index = lax.axis_index("row")
    column_index = lax.axis_index("col")
    (every_token,) = gather("row", 0, stream)
    tokens = every_token.shape[0]
    query_count = tokens // lax.axis_size("col")
    heads_here = query_weight.shape[1] // HD
    query_width = heads_here * HD
    pair_head = row_index * heads_here // (HEADS // KV_HEADS)
    whole_float = every_token.astype(jnp.float32)
    normed = (whole_float * attention_gain.astype(jnp.float32)).astype(jnp.bfloat16)
    pair_columns = lax.dynamic_slice_in_dim(pair_weight, pair_head * 2 * HD, 2 * HD, 1)
    query_rows, pair_sums, squares = scatter(
        "col",
        1,
        product(normed, query_weight),
        product(normed, pair_columns),
        square_sums(whole_float),
    )
    query_start = column_index * query_count
    row_scale = lax.rsqrt(squares[:, :1] / D + epsilon)
    positions = jnp.arange(tokens, dtype=jnp.int32)
    query_positions = query_start + jnp.arange(query_count, dtype=jnp.int32)
    queries = rotate((row_scale * query_rows).reshape(query_count, heads_here, HD), query_positions)
    pair_values = row_scale * pair_sums
    own_keys = rotate(pair_values[:, :HD].reshape(query_count, 1, HD), query_positions)[:, 0, :]
    own_values = pair_values[:, HD:].astype(jnp.bfloat16)
    key_rows, value_rows = gather("col", 2, own_keys, own_values)
    scores = jnp.einsum("qhd,kd->hqk", queries, key_rows, precision=lax.Precision.HIGHEST) * HD ** (
        -0.5
    )
    causal = query_positions[:, None] >= positions[None, :]
    scores = jnp.where(causal[None, :, :], scores, -1e30)
    largest = jnp.max(scores, axis=-1, keepdims=True)
    exponent = jnp.exp(scores - largest)
    attention = (exponent / jnp.sum(exponent, axis=-1, keepdims=True)).astype(jnp.bfloat16)
    mixture = jnp.einsum("hqk,kd->qhd", attention, value_rows, preferred_element_type=jnp.float32)
    heads_out = mixture.reshape(query_count, query_width).astype(jnp.bfloat16)
    (every_head,) = gather("col", 3, heads_out)
    (attention_rows,) = scatter("row", 4, product(every_head, out_weight))
    hidden_rows = (stream.astype(jnp.float32) + attention_rows).astype(jnp.bfloat16)
    (hidden_all,) = gather("row", 5, hidden_rows)
    hidden_float = hidden_all.astype(jnp.float32)
    unit_input = (hidden_float * unit_gain.astype(jnp.float32)).astype(jnp.bfloat16)
    gate_rows, square_rows, up_rows = scatter(
        "col",
        6,
        product(unit_input, gate_weight),
        square_sums(hidden_float),
        late=(unit_input, up_weight),
    )
    unit_scale = lax.rsqrt(square_rows[:, :1] / D + epsilon)
    gate_sums = unit_scale * gate_rows
    upward = unit_scale * up_rows
    (activated,) = gather("col", 7, (jax.nn.silu(gate_sums) * upward).astype(jnp.bfloat16))
    (down_rows,) = scatter("row", 8, product(activated, down_weight))
    return (hidden_rows.astype(jnp.float32) + down_rows).astype(jnp.bfloat16)


def solution(mesh):
    return jax.shard_map(
        on_device,
        mesh=mesh,
        in_specs=(
            P("row", "col"),
            P("col"),
            P("col", "row"),
            P("col", None),
            P("row", "col"),
            P("col"),
            P("col", "row"),
            P("col", "row"),
            P("row", "col"),
        ),
        out_specs=P("row", "col"),
        check_vma=False,
    )
```
